256 devices in a mesh: gx: 8 (over z), gy: 32 (over y, x, core).
Axes of the slice: x: 4, y: 4, z: 8, core: 2. Of those that a mesh axis runs over, the one named last changes fastest.
Arguments:
- rhs: float32 [4096, 8192], P('gx', 'gy'), may hold values from -6 to 6, as said below
- pressure: float32 [4096, 8192], P('gx', 'gy'), may hold values from -6 to 6
- wet_mask: int32 [4096, 8192], P('gx', 'gy'), may hold values 0 or 1
- bathy_class: int32 [4096, 8192], P('gx', 'gy'), may hold values from 0 to 7
Outputs:
- new_pressure: float32 [4096, 8192], P('gx', 'gy')
- final_residual: float32 [4096, 8192], P('gx', 'gy')
The draws below stay inside these ranges and needn't reach their ends.
Inputs may be any that keep to these rules, and one draw needn't show every extreme that they name: `rhs`: real-valued and rough from cell to cell.
All inputs are finite; a program needn't handle non-finite values. No bound on the sum of `wet_mask` on one device may be relied on, other than what follows from the above.
Results may differ from the reference program's by a relative error of at most 0.0003.
Values sent between devices are 32-bit elements; how exact they have to be, the bound alone decides.
A program may use at most 128 MiB of HBM per device.

```python
import jax
import jax.numpy as jnp

LEVELS = 4
SWEEPS = 12
NX = 4096
NY = 8192


def draw_rhs(key, part):
    return jnp.clip(jax.random.normal(key, (NX, NY), jnp.float32), -6.0, 6.0)


def touch_ends(values, key, smallest, top_value):
    place = [jax.random.randint(jax.random.fold_in(key, axis), (), 0, length) for axis, length in enumerate(values.shape)]
    longest = values.shape.index(max(values.shape))
    next_to = place[:longest] + [(place[longest] + 1) % values.shape[longest]] + place[longest + 1:]
    return values.at[tuple(place)].set(smallest).at[tuple(next_to)].set(top_value)


def level_of(rng, shape, split, low, largest):
    def one(position, blocks):
        draws = jax.random.uniform(jax.random.fold_in(jax.random.fold_in(rng, 6), position), (blocks,), jnp.float32, low / len(split), largest / len(split))
        return jnp.repeat(jnp.exp(draws), shape[position] // blocks).reshape((-1,) + (1,) * (len(shape) - position - 1))

    factor_of = one(*split[0])
    for cut in split[1:]:
        factor_of = factor_of * one(*cut)
    return factor_of


def normal_values(own_key, extent, spread, limit, split=(), kind=jnp.bfloat16):
    drawn = spread * jax.random.normal(own_key, extent, jnp.float32)
    if split:
        drawn = drawn * level_of(own_key, extent, split, -0.22, 0.18)
    return jnp.clip(drawn, -limit, limit).astype(kind)


def setup_inputs(seed: int = 0) -> dict:
    key_list = jax.random.split(jax.random.key(seed), 5)
    rhs = draw_rhs(jax.random.fold_in(key_list[4], 71), 0)
    pressure = normal_values(key_list[1], (NX, NY), 1.0, 6.0, ((0, 8), (1, 32)), jnp.float32)
    wet_mask = touch_ends((jax.random.randint(key_list[2], (NX, NY), 0, 8) < 7).astype(jnp.int32), jax.random.fold_in(key_list[2], 1), 0, 1)
    bathy_class = touch_ends(jax.random.randint(key_list[3], (NX, NY), 0, 8), jax.random.fold_in(key_list[3], 1), 0, 7).astype(jnp.int32)
    return dict(rhs=rhs, pressure=pressure, wet_mask=wet_mask, bathy_class=bathy_class)


damping = 0.01
relaxation = 0.8


def mean_blocks(field):
    height, width = field.shape
    return field.reshape(height // 2, 2, width // 2, 2).sum(axis=(1, 3)) * 0.25


def padded(field):
    return jnp.pad(field, 1)


def face_couplings(weight_pad, level_scale):
    middle = weight_pad[1:-1, 1:-1]
    to_north = level_scale * jnp.minimum(middle, weight_pad[:-2, 1:-1])
    to_south = level_scale * jnp.minimum(middle, weight_pad[2:, 1:-1])
    to_west = level_scale * jnp.minimum(middle, weight_pad[1:-1, :-2])
    to_east = level_scale * jnp.minimum(middle, weight_pad[1:-1, 2:])
    diagonal = damping + to_north + to_south + to_west + to_east
    return (to_north, to_south, to_west, to_east, diagonal)


def apply_operator(field_pad, coeffs):
    to_north, to_south, to_west, to_east, diagonal = coeffs
    middle = field_pad[1:-1, 1:-1]
    beside = to_north * field_pad[:-2, 1:-1] + to_south * field_pad[2:, 1:-1]
    beside = beside + to_west * field_pad[1:-1, :-2] + to_east * field_pad[1:-1, 2:]
    return diagonal * middle - beside


def jacobi_step(field_pad, source, coeffs):
    middle = field_pad[1:-1, 1:-1]
    return middle + relaxation * (source - apply_operator(field_pad, coeffs)) / coeffs[4]


def prolong(field):
    return jnp.repeat(jnp.repeat(field, 2, axis=0), 2, axis=1)


def reference(rhs, pressure, wet_mask, bathy_class):
    wet_cells = wet_mask.astype(jnp.float32)
    weight = wet_cells * (1.0 + 0.5 * bathy_class.astype(jnp.float32))
    source = wet_cells * rhs
    first_guess = wet_cells * pressure
    level_coeffs = []
    for level in range(LEVELS + 1):
        level_coeffs.append(face_couplings(padded(weight), 0.5 ** level))
        if level < LEVELS:
            weight = mean_blocks(weight)
    sources = [source]
    iterates = []
    iterate = jacobi_step(padded(first_guess), source, level_coeffs[0])
    for level in range(LEVELS):
        if level > 0:
            iterate = relaxation * sources[level] / level_coeffs[level][4]
        iterates.append(iterate)
        residual_now = sources[level] - apply_operator(padded(iterate), level_coeffs[level])
        sources.append(mean_blocks(residual_now))
    current = jnp.zeros_like(sources[LEVELS])
    for sweep_index in range(SWEEPS):
        current = jacobi_step(padded(current), sources[LEVELS], level_coeffs[LEVELS])
    for level in range(LEVELS - 1, -1, -1):
        summed = iterates[level] + prolong(current)
        current = jacobi_step(padded(summed), sources[level], level_coeffs[level])
    final_residual = source - apply_operator(padded(current), level_coeffs[0])
    return current, final_residual
```

```python
import functools

import jax
import jax.numpy as jnp
from jax import lax
from jax.experimental import pallas as pl
from jax.experimental.pallas import tpu as pltpu
from jax.sharding import PartitionSpec as P

LEVELS = 4
SWEEPS = 12
DAMPING = 0.01
RELAX = 0.8
MESH = pl.DeviceIdType.MESH

LANES = 128
HALO = 24
BASE = 8
CHUNK = 40


def lane_of(shape):
    return lax.broadcasted_iota(jnp.int32, shape, len(shape) - 1)


def from_west(xs):
    rolled = [pltpu.roll(x, 1, 1) for x in xs]
    if len(xs) == 1:
        return rolled
    edge = lane_of(xs[0].shape) == 0
    return [jnp.where(edge, rolled[k - 1], rolled[k]) for k in range(len(xs))]


def from_east(xs):
    rolled = [pltpu.roll(x, LANES - 1, 1) for x in xs]
    if len(xs) == 1:
        return rolled
    edge = lane_of(xs[0].shape) == LANES - 1
    return [jnp.where(edge, rolled[(k + 1) % len(xs)], rolled[k]) for k in range(len(xs))]


def column(shape, axis, first, wrap, total):
    lane = lax.broadcasted_iota(jnp.int32, shape, axis) + first
    return jnp.where(lane < wrap, lane, lane - total)


def split_dot(x, matrix):
    high = x.astype(jnp.bfloat16)
    rest = x - high.astype(jnp.float32)
    mid = rest.astype(jnp.bfloat16)
    low = (rest - mid.astype(jnp.float32)).astype(jnp.bfloat16)
    dot = functools.partial(jnp.dot, preferred_element_type=jnp.float32)
    return dot(high, matrix) + dot(mid, matrix) + dot(low, matrix)


class Level:
    def __init__(self, rows, cols, ext):
        self.ext = ext
        self.n = rows + 2 * ext
        self.steps = -(-self.n // 8) * 8
        self.alloc = self.steps + 2 * BASE
        self.k = -(-(cols + 2 * ext) // LANES)
        self.total = self.k * LANES
        self.wrap = (self.total + cols) // 2

    def columns(self, shape, axis, first=0):
        return column(shape, axis, first, self.wrap, self.total)


def edges_and_diagonal(wref, k_count, at, n):
    w = [wref[k, pl.ds(at, n), :] for k in range(k_count)]
    south = [jnp.minimum(w[k], wref[k, pl.ds(at + 1, n), :]) for k in range(k_count)]
    north = [jnp.minimum(w[k], wref[k, pl.ds(at - 1, n), :]) for k in range(k_count)]
    beside = from_east(w)
    east = [jnp.minimum(w[k], beside[k]) for k in range(k_count)]
    west = from_west(east)
    diagonal = [DAMPING + (south[k] + north[k]) + (east[k] + west[k]) for k in range(k_count)]
    return north, south, east, west, diagonal


def residual(field, sref, east_ref, south_ref, k_count, at, n):
    v = [field[k, pl.ds(at, n), :] for k in range(k_count)]
    beside = from_east(v)
    flow = [east_ref[k, pl.ds(at, n), :] * (beside[k] - v[k]) for k in range(k_count)]
    back = from_west(flow)
    out = []
    for k in range(k_count):
        down = south_ref[k, pl.ds(at, n), :] * (field[k, pl.ds(at + 1, n), :] - v[k])
        up = south_ref[k, pl.ds(at - 1, n), :] * (field[k, pl.ds(at - 1, n), :] - v[k])
        inner = sref[k, pl.ds(at, n), :] - DAMPING * v[k]
        out.append(inner + (flow[k] - back[k]) + (down + up))
    return out, v


def over_rows(rows, chunk, body):
    if rows == chunk:
        body(BASE)
        return

    def step(i, carry):
        body(pl.multiple_of(BASE + i * chunk, 8))
        return carry

    lax.fori_loop(0, rows // chunk, step, 0)


def kernel(
    grid_rows,
    grid_cols,
    levels,
    rhs_hbm,
    pressure_hbm,
    wet_hbm,
    bathy_hbm,
    out_ref,
    res_ref,
    rhs_in,
    pressure_in,
    wet_in,
    bathy_in,
    fields,
    pack_east,
    pack_west,
    got_west,
    got_east,
    *scratch,
):
    scratch = list(scratch)
    take = lambda count: [scratch.pop(0) for _ in range(count)]
    w_refs = [fields.at[0]] + take(3)
    s_refs = [fields.at[1]] + take(3)
    v_refs = take(4)
    inv_refs = take(4)
    east_refs = take(4)
    south_refs = take(4)
    u_refs = take(4)
    own, wide = take(2)
    in_sem, send_sem, recv_sem, send2_sem, recv2_sem = take(5)
    g_ref = fields.at[2]
    rows, cols = rhs_in.shape
    fine = levels[0]

    gx, gy = lax.axis_index("gx"), lax.axis_index("gy")
    north = lax.rem(gx + grid_rows - 1, grid_rows)
    south = lax.rem(gx + 1, grid_rows)
    west = lax.rem(gy + grid_cols - 1, grid_cols)
    east = lax.rem(gy + 1, grid_cols)
    around = [
        (gx, east),
        (gx, west),
        (south, gy),
        (north, gy),
        (south, east),
        (north, east),
        (south, west),
        (north, west),
    ]
    barrier = pltpu.get_barrier_semaphore()
    for device in around:
        pl.semaphore_signal(barrier, inc=1, device_id=device, device_id_type=MESH)

    loads = [
        pltpu.make_async_copy(src, dst, in_sem.at[i])
        for i, (src, dst) in enumerate(
            ((wet_hbm, wet_in), (bathy_hbm, bathy_in), (rhs_hbm, rhs_in), (pressure_hbm, pressure_in))
        )
    ]
    for load in loads:
        load.start()

    has_north = (gx > 0).astype(jnp.float32)
    has_south = (gx < grid_rows - 1).astype(jnp.float32)
    has_west = (gy > 0).astype(jnp.float32)
    has_east = (gy < grid_cols - 1).astype(jnp.float32)

    def clear(ref, level):
        for k in range(level.k):
            ref[k, 0:BASE, :] = jnp.zeros((BASE, LANES), jnp.float32)
            tail = level.alloc - BASE - level.n
            ref[k, BASE + level.n : level.alloc, :] = jnp.zeros((tail, LANES), jnp.float32)

    clear(g_ref, fine)
    for i, level in enumerate(levels):
        for refs in (w_refs, s_refs, v_refs, south_refs, u_refs):
            clear(refs[i], level)

    for load in loads:
        load.wait()

    first = BASE + HALO

    prep = 64
    lane = lane_of((prep, LANES))

    def prepare(i, carry):
        at = pl.multiple_of(i * prep, 8)
        to = pl.multiple_of(first + i * prep, 8)
        made = []
        for k in range(2):
            part = slice(k * LANES, (k + 1) * LANES)
            wet = wet_in[pl.ds(at, prep), part].astype(jnp.float32)
            bathy = bathy_in[pl.ds(at, prep), part].astype(jnp.float32)
            w = wet * (1.0 + 0.5 * bathy)
            s = wet * rhs_in[pl.ds(at, prep), part]
            g = wet * pressure_in[pl.ds(at, prep), part]
            fields[0, k, pl.ds(to, prep), :] = w
            fields[1, k, pl.ds(to, prep), :] = s
            fields[2, k, pl.ds(to, prep), :] = g
            made.append((w, s, g))
        w, s, g = made[1]
        packed = jnp.where(lane >= LANES - HALO, w, pltpu.roll(s, LANES - HALO, 1))
        pack_east[pl.ds(at, prep), :] = jnp.where(
            lane >= LANES - 2 * HALO, packed, pltpu.roll(g, LANES - 2 * HALO, 1)
        )
        w, s, g = made[0]
        packed = jnp.where(lane < HALO, w, pltpu.roll(s, HALO, 1))
        pack_west[pl.ds(at, prep), :] = jnp.where(lane < 2 * HALO, packed, pltpu.roll(g, 2 * HALO, 1))
        return carry

    lax.fori_loop(0, rows // prep, prepare, 0)

    pl.semaphore_wait(barrier, len(around))

    top = slice(BASE, BASE + HALO)
    middle = slice(first, first + rows)
    bottom = slice(first + rows, first + rows + HALO)
    head, tail = slice(0, HALO), slice(rows - HALO, rows)
    mine_head = slice(first, first + HALO)
    mine_tail = slice(first + rows - HALO, first + rows)
    strips = [
        (pack_east, got_west.at[middle]),
        (pack_west, got_east.at[middle]),
        (fields.at[:, 0:2, mine_tail], fields.at[:, 0:2, top]),
        (fields.at[:, 0:2, mine_head], fields.at[:, 0:2, bottom]),
        (pack_east.at[tail], got_west.at[top]),
        (pack_east.at[head], got_west.at[bottom]),
        (pack_west.at[tail], got_east.at[top]),
        (pack_west.at[head], got_east.at[bottom]),
    ]
    copies = [
        pltpu.make_async_remote_copy(
            src_ref=src,
            dst_ref=dst,
            send_sem=send_sem.at[i],
            recv_sem=recv_sem.at[i],
            device_id=around[i],
            device_id_type=MESH,
        )
        for i, (src, dst) in enumerate(strips)
    ]
    for copy in copies:
        copy.start()
    for copy in copies:
        copy.wait()

    part = 56
    lane_part = lane_of((part, LANES))

    def unpack(i, carry):
        at = pl.multiple_of(BASE + i * part, 8)
        a = got_west[pl.ds(at, part), :]
        b = got_east[pl.ds(at, part), :]
        left = lane_part >= LANES // 2
        w = jnp.where(lane_part < HALO, b * has_east, 0.0)
        fields[0, 2, pl.ds(at, part), :] = jnp.where(lane_part >= LANES - HALO, a * has_west, w)
        fields[1, 2, pl.ds(at, part), :] = jnp.where(
            left, pltpu.roll(a, HALO, 1), pltpu.roll(b, LANES - HALO, 1)
        )
        fields[2, 2, pl.ds(at, part), :] = jnp.where(
            left, pltpu.roll(a, 2 * HALO, 1), pltpu.roll(b, LANES - 2 * HALO, 1)
        )
        return carry

    lax.fori_loop(0, fine.n // part, unpack, 0)
    for k in range(3):
        fields[0, k, top, :] = fields[0, k, top, :] * has_north
        fields[0, k, bottom, :] = fields[0, k, bottom, :] * has_south

    def restrict_map(level, coarse_cols, k_in, first_in, scale):
        shape = (k_in * LANES, LANES)
        hit = (level.columns(shape, 0, first_in * LANES) >> 1) == coarse_cols(shape)
        return jnp.where(hit, scale, 0.0).astype(jnp.bfloat16)

    def restrict_plan(l):
        if l == 0:
            return [(0, 2, 0), (2, 1, 1)]
        return [(0, levels[l].k, 0)]

    def restrict(ref, l, start, count, scale, coarse_cols):
        out = []
        for k0, k_in, k_out in restrict_plan(l):
            sums = [
                ref[k, pl.ds(start, count, stride=2), :] + ref[k, pl.ds(start + 1, count, stride=2), :]
                for k in range(k0, k0 + k_in)
            ]
            x = sums[0] if k_in == 1 else jnp.concatenate(sums, axis=1)
            matrix = restrict_map(levels[l], functools.partial(coarse_cols, k_out), k_in, k0, scale)
            out.append(split_dot(x, matrix))
        return out

    def coarse_columns(l):
        if l == LEVELS - 1:
            return lambda k, shape: lax.broadcasted_iota(jnp.int32, shape, 1) & (cols // 2**LEVELS - 1)
        return lambda k, shape: levels[l + 1].columns(shape, 1, k * LANES)

    tile_rows = rows // 2**LEVELS

    def send_tile(f):
        half = tile_rows // 2
        all_rows, up_rows, down_rows = slice(0, tile_rows), slice(0, half), slice(half, tile_rows)
        mid, above, below = slice(half, half + tile_rows), slice(0, half), slice(half + tile_rows, 2 * tile_rows)
        plan = [
            (all_rows, 0, mid),
            (all_rows, 2, mid),
            (down_rows, 1, above),
            (up_rows, 1, below),
            (down_rows, 0, above),
            (up_rows, 0, below),
            (down_rows, 2, above),
            (up_rows, 2, below),
        ]
        out = [
            pltpu.make_async_remote_copy(
                src_ref=own.at[f, src],
                dst_ref=wide.at[f, which, dst],
                send_sem=send2_sem.at[f, i],
                recv_sem=recv2_sem.at[f, i],
                device_id=around[i],
                device_id_type=MESH,
            )
            for i, (src, which, dst) in enumerate(plan)
        ]
        for copy in out:
            copy.start()
        return out

    for l in range(LEVELS - 1):
        level = levels[l]
        made = restrict(w_refs[l], l, BASE, level.n // 2, 0.125, coarse_columns(l))
        for k in range(levels[l + 1].k):
            w_refs[l + 1][k, pl.ds(BASE, level.n // 2), :] = made[k]
    last = levels[LEVELS - 1]
    tile = restrict(
        w_refs[LEVELS - 1], LEVELS - 1, BASE + last.ext, tile_rows, 0.125, coarse_columns(LEVELS - 1)
    )[0]
    own[0, :, :] = tile
    wide[0, 1, pl.ds(tile_rows // 2, tile_rows), :] = tile
    weight_copies = send_tile(0)

    def chunk_of(level):
        return CHUNK if level.steps % CHUNK == 0 and level.k > 1 else level.steps

    for l in range(LEVELS):
        level = levels[l]
        k_count = level.k
        n = chunk_of(level)

        def smooth(at):
            up, down, right, left, diagonal = edges_and_diagonal(w_refs[l], k_count, at, n)
            for k in range(k_count):
                inverse = RELAX / diagonal[k]
                inv_refs[l][k, pl.ds(at, n), :] = inverse
                east_refs[l][k, pl.ds(at, n), :] = right[k]
                south_refs[l][k, pl.ds(at, n), :] = down[k]
                if l > 0:
                    v_refs[l][k, pl.ds(at, n), :] = inverse * s_refs[l][k, pl.ds(at, n), :]
            if l == 0:
                g = [g_ref[k, pl.ds(at, n), :] for k in range(k_count)]
                beside = from_east(g)
                flow = [right[k] * (beside[k] - g[k]) for k in range(k_count)]
                back = from_west(flow)
                for k in range(k_count):
                    below = down[k] * (g_ref[k, pl.ds(at + 1, n), :] - g[k])
                    above = up[k] * (g_ref[k, pl.ds(at - 1, n), :] - g[k])
                    inner = s_refs[0][k, pl.ds(at, n), :] - DAMPING * g[k]
                    total = inner + (flow[k] - back[k]) + (below + above)
                    v_refs[0][k, pl.ds(at, n), :] = g[k] + (RELAX / diagonal[k]) * total

        over_rows(level.steps, n, smooth)

        def to_residual(at):
            out, _ = residual(v_refs[l], s_refs[l], east_refs[l], south_refs[l], k_count, at, n)
            for k in range(k_count):
                u_refs[l][k, pl.ds(at, n), :] = out[k]

        over_rows(level.steps, n, to_residual)
        if l < LEVELS - 1:
            made = restrict(u_refs[l], l, BASE, level.n // 2, 0.25, coarse_columns(l))
            for k in range(levels[l + 1].k):
                s_refs[l + 1][k, pl.ds(BASE, level.n // 2), :] = made[k]
        else:
            tile = restrict(u_refs[l], l, BASE + last.ext, tile_rows, 0.25, coarse_columns(l))[0]
            own[1, :, :] = tile
            wide[1, 1, pl.ds(tile_rows // 2, tile_rows), :] = tile
    source_copies = send_tile(1)

    for copy in weight_copies:
        copy.wait()
    tile_cols = cols // 2**LEVELS
    wide_rows = 2 * tile_rows
    lane_wide = lane_of((wide_rows, LANES))
    row_wide = lax.broadcasted_iota(jnp.int32, (wide_rows, LANES), 0)

    def merged(f, a, b):
        x = jnp.where(lane_wide < 2 * tile_cols, wide[f, 2] * b, 0.0)
        x = jnp.where(lane_wide < tile_cols, wide[f, 1], x)
        return jnp.where(lane_wide >= LANES - tile_cols, wide[f, 0] * a, x)

    w = merged(0, has_west, has_east)
    w = jnp.where(row_wide < tile_rows // 2, w * has_north, w)
    w = jnp.where(row_wide >= tile_rows + tile_rows // 2, w * has_south, w)

    def roll_rows(x, shift):
        return pltpu.roll(x, shift % wide_rows, 0)

    c_south = jnp.minimum(w, roll_rows(w, -1))
    c_north = roll_rows(c_south, 1)
    c_east = jnp.minimum(w, pltpu.roll(w, LANES - 1, 1))
    c_west = pltpu.roll(c_east, 1, 1)
    inverse = RELAX / (DAMPING + (c_south + c_north) + (c_east + c_west))
    for copy in source_copies:
        copy.wait()
    source = merged(1, 1.0, 1.0) * inverse
    a_south, a_north, a_east, a_west = (c * inverse for c in (c_south, c_north, c_east, c_west))

    def sweep(current):
        rows_part = a_south * roll_rows(current, -1) + a_north * roll_rows(current, 1)
        lanes_part = a_east * pltpu.roll(current, LANES - 1, 1) + a_west * pltpu.roll(current, 1, 1)
        return ((1.0 - RELAX) * current + source) + (rows_part + lanes_part)

    current = source
    for _ in range(SWEEPS - 1):
        current = sweep(current)

    for l in range(LEVELS - 1, -1, -1):
        level = levels[l]
        k_count = level.k
        n = chunk_of(level)
        if l == LEVELS - 1:
            lead = (level.ext + 1) // 2
            count = (level.n + 2) // 2
            wide[0, 0, :, :] = current
            coarse = [wide[0, 0, pl.ds(tile_rows // 2 - lead, count), :]]
            start = BASE + level.ext - 2 * lead
            coarse_col = lambda shape: column(shape, 0, 0, LANES // 2, LANES)
            plan = [(0, 1, 0)]
        else:
            count = level.n // 2
            coarse = [v_refs[l + 1][k, pl.ds(BASE, count), :] for k in range(levels[l + 1].k)]
            start = BASE
            plan = [(0, 2, 0), (2, 1, 1)] if l == 0 else [(0, k_count, None)]
        for k0, k_out, k_from in plan:
            if l < LEVELS - 1:
                source_level = levels[l + 1]
                if k_from is None:
                    x = coarse[0] if len(coarse) == 1 else jnp.concatenate(coarse, axis=1)
                    first_lane = 0
                else:
                    x, first_lane = coarse[k_from], k_from * LANES
                coarse_col = lambda shape: source_level.columns(shape, 0, first_lane)
            else:
                x = coarse[0]
            shape = (x.shape[1], k_out * LANES)
            hit = (level.columns(shape, 1, k0 * LANES) >> 1) == coarse_col(shape)
            spread = split_dot(x, jnp.where(hit, 1.0, 0.0).astype(jnp.bfloat16))
            for k in range(k_out):
                add = spread[:, k * LANES : (k + 1) * LANES]
                for side in range(2):
                    at = pl.ds(start + side, count, stride=2)
                    u_refs[l][k0 + k, at, :] = v_refs[l][k0 + k, at, :] + add

        def correct(at):
            out, v = residual(u_refs[l], s_refs[l], east_refs[l], south_refs[l], k_count, at, n)
            for k in range(k_count):
                v_refs[l][k, pl.ds(at, n), :] = v[k] + inv_refs[l][k, pl.ds(at, n), :] * out[k]

        over_rows(level.steps, n, correct)

    def finish(i, carry):
        at = pl.multiple_of(first + i * 32, 8)
        to = pl.multiple_of(i * 32, 8)
        out, v = residual(v_refs[0], s_refs[0], east_refs[0], south_refs[0], 3, at, 32)
        for k in range(2):
            out_ref[pl.ds(to, 32), k * LANES : (k + 1) * LANES] = v[k]
            res_ref[pl.ds(to, 32), k * LANES : (k + 1) * LANES] = out[k]
        return carry

    lax.fori_loop(0, rows // 32, finish, 0)


def local(grid_rows, grid_cols, rhs, pressure, wet_mask, bathy_class):
    rows, cols = rhs.shape
    levels = [Level(rows >> l, cols >> l, HALO >> l) for l in range(LEVELS)]
    f32 = jnp.float32
    vmem = lambda *shape: pltpu.VMEM(shape, f32)
    per_level = [vmem(level.k, level.alloc, LANES) for level in levels]
    tile_rows = rows // 2**LEVELS
    scratch = [
        vmem(rows, cols),
        vmem(rows, cols),
        pltpu.VMEM((rows, cols), jnp.int32),
        pltpu.VMEM((rows, cols), jnp.int32),
        vmem(3, levels[0].k, levels[0].alloc, LANES),
        vmem(rows, LANES),
        vmem(rows, LANES),
        vmem(levels[0].alloc, LANES),
        vmem(levels[0].alloc, LANES),
        *per_level[1:],
        *per_level[1:],
        *per_level,
        *per_level,
        *per_level,
        *per_level,
        *per_level,
        vmem(2, tile_rows, LANES),
        vmem(2, 3, 2 * tile_rows, LANES),
        pltpu.SemaphoreType.DMA((4,)),
        pltpu.SemaphoreType.DMA((8,)),
        pltpu.SemaphoreType.DMA((8,)),
        pltpu.SemaphoreType.DMA((2, 8)),
        pltpu.SemaphoreType.DMA((2, 8)),
    ]
    return pl.pallas_call(
        functools.partial(kernel, grid_rows, grid_cols, levels),
        out_shape=[jax.ShapeDtypeStruct((rows, cols), f32)] * 2,
        in_specs=[pl.BlockSpec(memory_space=pl.ANY)] * 4,
        out_specs=[pl.BlockSpec(memory_space=pltpu.VMEM)] * 2,
        scratch_shapes=scratch,
        compiler_params=pltpu.CompilerParams(
            collective_id=0, has_side_effects=True, vmem_limit_bytes=48 * 1024 * 1024
        ),
    )(rhs, pressure, wet_mask, bathy_class)


def solution(mesh):
    placed = P("gx", "gy")
    body = functools.partial(local, mesh.shape["gx"], mesh.shape["gy"])
    return jax.shard_map(
        lambda *args: tuple(body(*args)),
        mesh=mesh,
        in_specs=(placed,) * 4,
        out_specs=(placed,) * 2,
        check_vma=False,
    )
```

```python
import functools

import jax
import jax.numpy as jnp
from jax import lax
from jax.experimental import pallas as pl
from jax.experimental.pallas import tpu as pltpu
from jax.sharding import PartitionSpec as P

LEVELS = 4
SWEEPS = 12
DAMPING = 0.01
RELAX = 0.8
MESH = pl.DeviceIdType.MESH

LANES = 128
HALO = 24
BASE = 8


def lane_of(shape):
    return lax.broadcasted_iota(jnp.int32, shape, len(shape) - 1)


def from_west(xs):
    rolled = [pltpu.roll(x, 1, 1) for x in xs]
    if len(xs) == 1:
        return rolled
    edge = lane_of(xs[0].shape) == 0
    return [jnp.where(edge, rolled[k - 1], rolled[k]) for k in range(len(xs))]


def from_east(xs):
    rolled = [pltpu.roll(x, LANES - 1, 1) for x in xs]
    if len(xs) == 1:
        return rolled
    edge = lane_of(xs[0].shape) == LANES - 1
    return [jnp.where(edge, rolled[(k + 1) % len(xs)], rolled[k]) for k in range(len(xs))]


def column(shape, axis, first, wrap, total):
    lane = lax.broadcasted_iota(jnp.int32, shape, axis) + first
    return jnp.where(lane < wrap, lane, lane - total)


def split_dot(x, matrix):
    high = x.astype(jnp.bfloat16)
    rest = x - high.astype(jnp.float32)
    mid = rest.astype(jnp.bfloat16)
    low = (rest - mid.astype(jnp.float32)).astype(jnp.bfloat16)
    dot = functools.partial(jnp.dot, preferred_element_type=jnp.float32)
    return dot(high, matrix) + dot(mid, matrix) + dot(low, matrix)


class Level:
    def __init__(self, rows, cols, ext):
        self.ext = ext
        self.n = rows + 2 * ext
        self.steps = -(-self.n // 8) * 8
        self.alloc = self.steps + 2 * BASE
        self.k = -(-(cols + 2 * ext) // LANES)
        self.total = self.k * LANES
        self.wrap = (self.total + cols) // 2

    def columns(self, shape, axis, first=0):
        return column(shape, axis, first, self.wrap, self.total)


def edges_and_diagonal(wref, k_count, at, n):
    w = [wref[k, pl.ds(at, n), :] for k in range(k_count)]
    south = [jnp.minimum(w[k], wref[k, pl.ds(at + 1, n), :]) for k in range(k_count)]
    north = [jnp.minimum(w[k], wref[k, pl.ds(at - 1, n), :]) for k in range(k_count)]
    beside = from_east(w)
    east = [jnp.minimum(w[k], beside[k]) for k in range(k_count)]
    west = from_west(east)
    diagonal = [DAMPING + (south[k] + north[k]) + (east[k] + west[k]) for k in range(k_count)]
    return north, south, east, west, diagonal


def residual(field, sref, east_ref, south_ref, k_count, at, n):
    v = [field[k, pl.ds(at, n), :] for k in range(k_count)]
    beside = from_east(v)
    flow = [east_ref[k, pl.ds(at, n), :] * (beside[k] - v[k]) for k in range(k_count)]
    back = from_west(flow)
    out = []
    for k in range(k_count):
        down = south_ref[k, pl.ds(at, n), :] * (field[k, pl.ds(at + 1, n), :] - v[k])
        up = south_ref[k, pl.ds(at - 1, n), :] * (field[k, pl.ds(at - 1, n), :] - v[k])
        inner = sref[k, pl.ds(at, n), :] - DAMPING * v[k]
        out.append(inner + (flow[k] - back[k]) + (down + up))
    return out, v


def over_rows(rows, chunk, body):
    if rows == chunk:
        body(BASE)
        return

    def step(i, carry):
        body(pl.multiple_of(BASE + i * chunk, 8))
        return carry

    lax.fori_loop(0, rows // chunk, step, 0)


def kernel(
    grid_rows,
    grid_cols,
    levels,
    rhs_hbm,
    pressure_hbm,
    wet_hbm,
    bathy_hbm,
    out_ref,
    res_ref,
    rhs_in,
    pressure_in,
    wet_in,
    bathy_in,
    fields,
    pack_east,
    pack_west,
    got_west,
    got_east,
    *scratch,
):
    scratch = list(scratch)
    take = lambda count: [scratch.pop(0) for _ in range(count)]
    w_refs = [fields.at[0]] + take(3)
    s_refs = [fields.at[1]] + take(3)
    v_refs = take(4)
    inv_refs = take(4)
    east_refs = take(4)
    south_refs = take(4)
    u_refs = take(4)
    own, wide = take(2)
    in_sem, send_sem, recv_sem, send2_sem, recv2_sem = take(5)
    g_ref = fields.at[2]
    rows, cols = rhs_in.shape
    fine = levels[0]

    gx, gy = lax.axis_index("gx"), lax.axis_index("gy")
    north = lax.rem(gx + grid_rows - 1, grid_rows)
    south = lax.rem(gx + 1, grid_rows)
    west = lax.rem(gy + grid_cols - 1, grid_cols)
    east = lax.rem(gy + 1, grid_cols)
    around = [
        (gx, east),
        (gx, west),
        (south, gy),
        (north, gy),
        (south, east),
        (north, east),
        (south, west),
        (north, west),
    ]
    barrier = pltpu.get_barrier_semaphore()
    for device in around:
        pl.semaphore_signal(barrier, inc=1, device_id=device, device_id_type=MESH)

    loads = [
        pltpu.make_async_copy(src, dst, in_sem.at[i])
        for i, (src, dst) in enumerate(
            ((wet_hbm, wet_in), (bathy_hbm, bathy_in), (rhs_hbm, rhs_in), (pressure_hbm, pressure_in))
        )
    ]
    for load in loads:
        load.start()

    has_north = (gx > 0).astype(jnp.float32)
    has_south = (gx < grid_rows - 1).astype(jnp.float32)
    has_west = (gy > 0).astype(jnp.float32)
    has_east = (gy < grid_cols - 1).astype(jnp.float32)

    def clear(ref, level):
        for k in range(level.k):
            ref[k, 0:BASE, :] = jnp.zeros((BASE, LANES), jnp.float32)
            tail = level.alloc - BASE - level.n
            ref[k, BASE + level.n : level.alloc, :] = jnp.zeros((tail, LANES), jnp.float32)

    clear(g_ref, fine)
    for i, level in enumerate(levels):
        for refs in (w_refs, s_refs, v_refs, south_refs, u_refs):
            clear(refs[i], level)

    for load in loads:
        load.wait()

    first = BASE + HALO

    prep = rows
    lane = lane_of((prep, LANES))

    def prepare(i, carry):
        at = i * prep
        to = first + i * prep
        made = []
        for k in range(2):
            part = slice(k * LANES, (k + 1) * LANES)
            wet = wet_in[pl.ds(at, prep), part].astype(jnp.float32)
            bathy = bathy_in[pl.ds(at, prep), part].astype(jnp.float32)
            w = wet * (1.0 + 0.5 * bathy)
            s = wet * rhs_in[pl.ds(at, prep), part]
            g = wet * pressure_in[pl.ds(at, prep), part]
            fields[0, k, pl.ds(to, prep), :] = w
            fields[1, k, pl.ds(to, prep), :] = s
            fields[2, k, pl.ds(to, prep), :] = g
            made.append((w, s, g))
        w, s, g = made[1]
        packed = jnp.where(lane >= LANES - HALO, w, pltpu.roll(s, LANES - HALO, 1))
        pack_east[pl.ds(at, prep), :] = jnp.where(
            lane >= LANES - 2 * HALO, packed, pltpu.roll(g, LANES - 2 * HALO, 1)
        )
        w, s, g = made[0]
        packed = jnp.where(lane < HALO, w, pltpu.roll(s, HALO, 1))
        pack_west[pl.ds(at, prep), :] = jnp.where(lane < 2 * HALO, packed, pltpu.roll(g, 2 * HALO, 1))
        return carry

    prepare(0, 0)

    pl.semaphore_wait(barrier, len(around))

    top = slice(BASE, BASE + HALO)
    middle = slice(first, first + rows)
    bottom = slice(first + rows, first + rows + HALO)
    head, tail = slice(0, HALO), slice(rows - HALO, rows)
    mine_head = slice(first, first + HALO)
    mine_tail = slice(first + rows - HALO, first + rows)
    strips = [
        (pack_east, got_west.at[middle]),
        (pack_west, got_east.at[middle]),
        (fields.at[:, 0:2, mine_tail], fields.at[:, 0:2, top]),
        (fields.at[:, 0:2, mine_head], fields.at[:, 0:2, bottom]),
        (pack_east.at[tail], got_west.at[top]),
        (pack_east.at[head], got_west.at[bottom]),
        (pack_west.at[tail], got_east.at[top]),
        (pack_west.at[head], got_east.at[bottom]),
    ]
    copies = [
        pltpu.make_async_remote_copy(
            src_ref=src,
            dst_ref=dst,
            send_sem=send_sem.at[i],
            recv_sem=recv_sem.at[i],
            device_id=around[i],
            device_id_type=MESH,
        )
        for i, (src, dst) in enumerate(strips)
    ]
    for copy in copies:
        copy.start()
    for copy in copies:
        copy.wait()

    part = fine.n
    lane_part = lane_of((part, LANES))

    def unpack(i, carry):
        at = BASE + i * part
        a = got_west[pl.ds(at, part), :]
        b = got_east[pl.ds(at, part), :]
        left = lane_part >= LANES // 2
        w = jnp.where(lane_part < HALO, b * has_east, 0.0)
        fields[0, 2, pl.ds(at, part), :] = jnp.where(lane_part >= LANES - HALO, a * has_west, w)
        fields[1, 2, pl.ds(at, part), :] = jnp.where(
            left, pltpu.roll(a, HALO, 1), pltpu.roll(b, LANES - HALO, 1)
        )
        fields[2, 2, pl.ds(at, part), :] = jnp.where(
            left, pltpu.roll(a, 2 * HALO, 1), pltpu.roll(b, LANES - 2 * HALO, 1)
        )
        return carry

    unpack(0, 0)
    for k in range(3):
        fields[0, k, top, :] = fields[0, k, top, :] * has_north
        fields[0, k, bottom, :] = fields[0, k, bottom, :] * has_south

    def restrict_map(level, coarse_cols, k_in, first_in, scale):
        shape = (k_in * LANES, LANES)
        hit = (level.columns(shape, 0, first_in * LANES) >> 1) == coarse_cols(shape)
        return jnp.where(hit, scale, 0.0).astype(jnp.bfloat16)

    def restrict_plan(l):
        if l == 0:
            return [(0, 2, 0), (2, 1, 1)]
        return [(0, levels[l].k, 0)]

    def restrict(ref, l, start, count, scale, coarse_cols):
        out = []
        for k0, k_in, k_out in restrict_plan(l):
            sums = [
                ref[k, pl.ds(start, count, stride=2), :] + ref[k, pl.ds(start + 1, count, stride=2), :]
                for k in range(k0, k0 + k_in)
            ]
            x = sums[0] if k_in == 1 else jnp.concatenate(sums, axis=1)
            matrix = restrict_map(levels[l], functools.partial(coarse_cols, k_out), k_in, k0, scale)
            out.append(split_dot(x, matrix))
        return out

    def coarse_columns(l):
        if l == LEVELS - 1:
            return lambda k, shape: lax.broadcasted_iota(jnp.int32, shape, 1) & (cols // 2**LEVELS - 1)
        return lambda k, shape: levels[l + 1].columns(shape, 1, k * LANES)

    tile_rows = rows // 2**LEVELS

    def send_tile(f):
        half = tile_rows // 2
        all_rows, up_rows, down_rows = slice(0, tile_rows), slice(0, half), slice(half, tile_rows)
        mid, above, below = slice(half, half + tile_rows), slice(0, half), slice(half + tile_rows, 2 * tile_rows)
        plan = [
            (all_rows, 0, mid),
            (all_rows, 2, mid),
            (down_rows, 1, above),
            (up_rows, 1, below),
            (down_rows, 0, above),
            (up_rows, 0, below),
            (down_rows, 2, above),
            (up_rows, 2, below),
        ]
        out = [
            pltpu.make_async_remote_copy(
                src_ref=own.at[f, src],
                dst_ref=wide.at[f, which, dst],
                send_sem=send2_sem.at[f, i],
                recv_sem=recv2_sem.at[f, i],
                device_id=around[i],
                device_id_type=MESH,
            )
            for i, (src, which, dst) in enumerate(plan)
        ]
        for copy in out:
            copy.start()
        return out

    for l in range(LEVELS - 1):
        level = levels[l]
        made = restrict(w_refs[l], l, BASE, level.n // 2, 0.125, coarse_columns(l))
        for k in range(levels[l + 1].k):
            w_refs[l + 1][k, pl.ds(BASE, level.n // 2), :] = made[k]
    last = levels[LEVELS - 1]
    tile = restrict(
        w_refs[LEVELS - 1], LEVELS - 1, BASE + last.ext, tile_rows, 0.125, coarse_columns(LEVELS - 1)
    )[0]
    own[0, :, :] = tile
    wide[0, 1, pl.ds(tile_rows // 2, tile_rows), :] = tile
    weight_copies = send_tile(0)

    def chunk_of(level):
        return level.steps

    for l in range(LEVELS):
        level = levels[l]
        k_count = level.k
        n = chunk_of(level)

        def smooth(at):
            up, down, right, left, diagonal = edges_and_diagonal(w_refs[l], k_count, at, n)
            for k in range(k_count):
                inverse = RELAX / diagonal[k]
                inv_refs[l][k, pl.ds(at, n), :] = inverse
                east_refs[l][k, pl.ds(at, n), :] = right[k]
                south_refs[l][k, pl.ds(at, n), :] = down[k]
                if l > 0:
                    v_refs[l][k, pl.ds(at, n), :] = inverse * s_refs[l][k, pl.ds(at, n), :]
            if l == 0:
                g = [g_ref[k, pl.ds(at, n), :] for k in range(k_count)]
                beside = from_east(g)
                flow = [right[k] * (beside[k] - g[k]) for k in range(k_count)]
                back = from_west(flow)
                for k in range(k_count):
                    below = down[k] * (g_ref[k, pl.ds(at + 1, n), :] - g[k])
                    above = up[k] * (g_ref[k, pl.ds(at - 1, n), :] - g[k])
                    inner = s_refs[0][k, pl.ds(at, n), :] - DAMPING * g[k]
                    total = inner + (flow[k] - back[k]) + (below + above)
                    v_refs[0][k, pl.ds(at, n), :] = g[k] + (RELAX / diagonal[k]) * total

        over_rows(level.steps, n, smooth)

        def to_residual(at):
            out, _ = residual(v_refs[l], s_refs[l], east_refs[l], south_refs[l], k_count, at, n)
            for k in range(k_count):
                u_refs[l][k, pl.ds(at, n), :] = out[k]

        over_rows(level.steps, n, to_residual)
        if l < LEVELS - 1:
            made = restrict(u_refs[l], l, BASE, level.n // 2, 0.25, coarse_columns(l))
            for k in range(levels[l + 1].k):
                s_refs[l + 1][k, pl.ds(BASE, level.n // 2), :] = made[k]
        else:
            tile = restrict(u_refs[l], l, BASE + last.ext, tile_rows, 0.25, coarse_columns(l))[0]
            own[1, :, :] = tile
            wide[1, 1, pl.ds(tile_rows // 2, tile_rows), :] = tile
    source_copies = send_tile(1)

    for copy in weight_copies:
        copy.wait()
    tile_cols = cols // 2**LEVELS
    wide_rows = 2 * tile_rows
    lane_wide = lane_of((wide_rows, LANES))
    row_wide = lax.broadcasted_iota(jnp.int32, (wide_rows, LANES), 0)

    def merged(f, a, b):
        x = jnp.where(lane_wide < 2 * tile_cols, wide[f, 2] * b, 0.0)
        x = jnp.where(lane_wide < tile_cols, wide[f, 1], x)
        return jnp.where(lane_wide >= LANES - tile_cols, wide[f, 0] * a, x)

    w = merged(0, has_west, has_east)
    w = jnp.where(row_wide < tile_rows // 2, w * has_north, w)
    w = jnp.where(row_wide >= tile_rows + tile_rows // 2, w * has_south, w)

    def roll_rows(x, shift):
        return pltpu.roll(x, shift % wide_rows, 0)

    c_south = jnp.minimum(w, roll_rows(w, -1))
    c_north = roll_rows(c_south, 1)
    c_east = jnp.minimum(w, pltpu.roll(w, LANES - 1, 1))
    c_west = pltpu.roll(c_east, 1, 1)
    inverse = RELAX / (DAMPING + (c_south + c_north) + (c_east + c_west))
    for copy in source_copies:
        copy.wait()
    source = merged(1, 1.0, 1.0) * inverse
    a_south, a_north, a_east, a_west = (c * inverse for c in (c_south, c_north, c_east, c_west))

    def sweep(current):
        rows_part = a_south * roll_rows(current, -1) + a_north * roll_rows(current, 1)
        lanes_part = a_east * pltpu.roll(current, LANES - 1, 1) + a_west * pltpu.roll(current, 1, 1)
        return ((1.0 - RELAX) * current + source) + (rows_part + lanes_part)

    current = source
    for _ in range(SWEEPS - 1):
        current = sweep(current)

    for l in range(LEVELS - 1, -1, -1):
        level = levels[l]
        k_count = level.k
        n = chunk_of(level)
        if l == LEVELS - 1:
            lead = (level.ext + 1) // 2
            count = (level.n + 2) // 2
            wide[0, 0, :, :] = current
            coarse = [wide[0, 0, pl.ds(tile_rows // 2 - lead, count), :]]
            start = BASE + level.ext - 2 * lead
            coarse_col = lambda shape: column(shape, 0, 0, LANES // 2, LANES)
            plan = [(0, 1, 0)]
        else:
            count = level.n // 2
            coarse = [v_refs[l + 1][k, pl.ds(BASE, count), :] for k in range(levels[l + 1].k)]
            start = BASE
            plan = [(0, 2, 0), (2, 1, 1)] if l == 0 else [(0, k_count, None)]
        for k0, k_out, k_from in plan:
            if l < LEVELS - 1:
                source_level = levels[l + 1]
                if k_from is None:
                    x = coarse[0] if len(coarse) == 1 else jnp.concatenate(coarse, axis=1)
                    first_lane = 0
                else:
                    x, first_lane = coarse[k_from], k_from * LANES
                coarse_col = lambda shape: source_level.columns(shape, 0, first_lane)
            else:
                x = coarse[0]
            shape = (x.shape[1], k_out * LANES)
            hit = (level.columns(shape, 1, k0 * LANES) >> 1) == coarse_col(shape)
            spread = split_dot(x, jnp.where(hit, 1.0, 0.0).astype(jnp.bfloat16))
            for k in range(k_out):
                add = spread[:, k * LANES : (k + 1) * LANES]
                for side in range(2):
                    at = pl.ds(start + side, count, stride=2)
                    u_refs[l][k0 + k, at, :] = v_refs[l][k0 + k, at, :] + add

        def correct(at):
            out, v = residual(u_refs[l], s_refs[l], east_refs[l], south_refs[l], k_count, at, n)
            for k in range(k_count):
                v_refs[l][k, pl.ds(at, n), :] = v[k] + inv_refs[l][k, pl.ds(at, n), :] * out[k]

        over_rows(level.steps, n, correct)

    def finish(i, carry):
        at = first + i * rows
        to = i * rows
        out, v = residual(v_refs[0], s_refs[0], east_refs[0], south_refs[0], 3, at, rows)
        for k in range(2):
            out_ref[pl.ds(to, rows), k * LANES : (k + 1) * LANES] = v[k]
            res_ref[pl.ds(to, rows), k * LANES : (k + 1) * LANES] = out[k]
        return carry

    finish(0, 0)


def local(grid_rows, grid_cols, rhs, pressure, wet_mask, bathy_class):
    rows, cols = rhs.shape
    levels = [Level(rows >> l, cols >> l, HALO >> l) for l in range(LEVELS)]
    f32 = jnp.float32
    vmem = lambda *shape: pltpu.VMEM(shape, f32)
    per_level = [vmem(level.k, level.alloc, LANES) for level in levels]
    tile_rows = rows // 2**LEVELS
    scratch = [
        vmem(rows, cols),
        vmem(rows, cols),
        pltpu.VMEM((rows, cols), jnp.int32),
        pltpu.VMEM((rows, cols), jnp.int32),
        vmem(3, levels[0].k, levels[0].alloc, LANES),
        vmem(rows, LANES),
        vmem(rows, LANES),
        vmem(levels[0].alloc, LANES),
        vmem(levels[0].alloc, LANES),
        *per_level[1:],
        *per_level[1:],
        *per_level,
        *per_level,
        *per_level,
        *per_level,
        *per_level,
        vmem(2, tile_rows, LANES),
        vmem(2, 3, 2 * tile_rows, LANES),
        pltpu.SemaphoreType.DMA((4,)),
        pltpu.SemaphoreType.DMA((8,)),
        pltpu.SemaphoreType.DMA((8,)),
        pltpu.SemaphoreType.DMA((2, 8)),
        pltpu.SemaphoreType.DMA((2, 8)),
    ]
    return pl.pallas_call(
        functools.partial(kernel, grid_rows, grid_cols, levels),
        out_shape=[jax.ShapeDtypeStruct((rows, cols), f32)] * 2,
        in_specs=[pl.BlockSpec(memory_space=pl.ANY)] * 4,
        out_specs=[pl.BlockSpec(memory_space=pltpu.VMEM)] * 2,
        scratch_shapes=scratch,
        compiler_params=pltpu.CompilerParams(
            collective_id=0, has_side_effects=True, vmem_limit_bytes=62 * 1024 * 1024
        ),
    )(rhs, pressure, wet_mask, bathy_class)


def solution(mesh):
    placed = P("gx", "gy")
    body = functools.partial(local, mesh.shape["gx"], mesh.shape["gy"])
    return jax.shard_map(
        lambda *args: tuple(body(*args)),
        mesh=mesh,
        in_specs=(placed,) * 4,
        out_specs=(placed,) * 2,
        check_vma=False,
    )
```

```python
import functools

import jax
import jax.numpy as jnp
from jax import lax
from jax.experimental import pallas as pl
from jax.experimental.pallas import tpu as pltpu
from jax.sharding import PartitionSpec as P

LEVELS = 4
SWEEPS = 12
DAMPING = 0.01
RELAX = 0.8
MESH = pl.DeviceIdType.MESH

LANES = 128
HALO = 24
PIECES = 2
BASE = 8


def lane_of(shape):
    return lax.broadcasted_iota(jnp.int32, shape, len(shape) - 1)


def from_west(xs):
    rolled = [pltpu.roll(x, 1, 1) for x in xs]
    if len(xs) == 1:
        return rolled
    edge = lane_of(xs[0].shape) == 0
    return [jnp.where(edge, rolled[k - 1], rolled[k]) for k in range(len(xs))]


def from_east(xs):
    rolled = [pltpu.roll(x, LANES - 1, 1) for x in xs]
    if len(xs) == 1:
        return rolled
    edge = lane_of(xs[0].shape) == LANES - 1
    return [jnp.where(edge, rolled[(k + 1) % len(xs)], rolled[k]) for k in range(len(xs))]


def column(shape, axis, first, wrap, total):
    lane = lax.broadcasted_iota(jnp.int32, shape, axis) + first
    return jnp.where(lane < wrap, lane, lane - total)


def split_dot(x, matrix):
    high = x.astype(jnp.bfloat16)
    rest = x - high.astype(jnp.float32)
    mid = rest.astype(jnp.bfloat16)
    low = (rest - mid.astype(jnp.float32)).astype(jnp.bfloat16)
    dot = functools.partial(jnp.dot, preferred_element_type=jnp.float32)
    return dot(high, matrix) + dot(mid, matrix) + dot(low, matrix)


class Level:
    def __init__(self, rows, cols, ext):
        self.ext = ext
        self.n = rows + 2 * ext
        self.steps = -(-self.n // 8) * 8
        self.alloc = self.steps + 2 * BASE
        self.k = -(-(cols + 2 * ext) // LANES)
        self.total = self.k * LANES
        self.wrap = (self.total + cols) // 2

    def columns(self, shape, axis, first=0):
        return column(shape, axis, first, self.wrap, self.total)


def edges_and_diagonal(wref, k_count, at, n):
    w = [wref[k, pl.ds(at, n), :] for k in range(k_count)]
    south = [jnp.minimum(w[k], wref[k, pl.ds(at + 1, n), :]) for k in range(k_count)]
    north = [jnp.minimum(w[k], wref[k, pl.ds(at - 1, n), :]) for k in range(k_count)]
    beside = from_east(w)
    east = [jnp.minimum(w[k], beside[k]) for k in range(k_count)]
    west = from_west(east)
    diagonal = [DAMPING + (south[k] + north[k]) + (east[k] + west[k]) for k in range(k_count)]
    return north, south, east, west, diagonal


def residual(field, sref, east_ref, south_ref, k_count, at, n):
    v = [field[k, pl.ds(at, n), :] for k in range(k_count)]
    beside = from_east(v)
    flow = [east_ref[k, pl.ds(at, n), :] * (beside[k] - v[k]) for k in range(k_count)]
    back = from_west(flow)
    out = []
    for k in range(k_count):
        down = south_ref[k, pl.ds(at, n), :] * (field[k, pl.ds(at + 1, n), :] - v[k])
        up = south_ref[k, pl.ds(at - 1, n), :] * (field[k, pl.ds(at - 1, n), :] - v[k])
        inner = sref[k, pl.ds(at, n), :] - DAMPING * v[k]
        out.append(inner + (flow[k] - back[k]) + (down + up))
    return out, v


def over_rows(rows, chunk, body):
    if rows == chunk:
        body(BASE)
        return

    def step(i, carry):
        body(pl.multiple_of(BASE + i * chunk, 8))
        return carry

    lax.fori_loop(0, rows // chunk, step, 0)


def kernel(
    grid_rows,
    grid_cols,
    levels,
    rhs_hbm,
    pressure_hbm,
    wet_hbm,
    bathy_hbm,
    field_out,
    fields,
    east_out,
    south_out,
    rhs_in,
    pressure_in,
    wet_in,
    bathy_in,
    pack_east,
    pack_west,
    got_west,
    got_east,
    *scratch,
):
    scratch = list(scratch)
    take = lambda count: [scratch.pop(0) for _ in range(count)]
    w_refs = [fields.at[0]] + take(3)
    s_refs = [fields.at[1]] + take(3)
    v_refs = [field_out] + take(3)
    inv_refs = take(4)
    east_refs = [east_out] + take(3)
    south_refs = [south_out] + take(3)
    u_refs = take(4)
    own, wide = take(2)
    in_sem, send_sem, recv_sem, send2_sem, recv2_sem = take(5)
    g_ref = fields.at[2]
    rows, cols = rhs_in.shape
    fine = levels[0]

    gx, gy = lax.axis_index("gx"), lax.axis_index("gy")
    north = lax.rem(gx + grid_rows - 1, grid_rows)
    south = lax.rem(gx + 1, grid_rows)
    west = lax.rem(gy + grid_cols - 1, grid_cols)
    east = lax.rem(gy + 1, grid_cols)
    around = [
        (gx, east),
        (gx, west),
        (south, gy),
        (north, gy),
        (south, east),
        (north, east),
        (south, west),
        (north, west),
    ]
    at_north, at_south = gx == 0, gx == grid_rows - 1
    at_west, at_east = gy == 0, gy == grid_cols - 1
    inside = lambda *edges: functools.reduce(jnp.logical_and, [jnp.logical_not(edge) for edge in edges])
    exists = [
        inside(at_east),
        inside(at_west),
        inside(at_south),
        inside(at_north),
        inside(at_south, at_east),
        inside(at_north, at_east),
        inside(at_south, at_west),
        inside(at_north, at_west),
    ]
    opposite = [1, 0, 3, 2, 7, 6, 5, 4]
    barrier = pltpu.get_barrier_semaphore()
    for i, device in enumerate(around):

        @pl.when(exists[i])
        def _():
            pl.semaphore_signal(barrier, inc=1, device_id=device, device_id_type=MESH)

    def start_all(copies):
        for i, copy in enumerate(copies):
            pl.when(exists[i])(copy.start)

    def wait_all(copies):
        for i, copy in enumerate(copies):
            pl.when(exists[opposite[i]])(copy.wait_recv)
        for i, copy in enumerate(copies):
            pl.when(exists[i])(copy.wait_send)

    loads = [
        pltpu.make_async_copy(src, dst, in_sem.at[i])
        for i, (src, dst) in enumerate(
            ((wet_hbm, wet_in), (bathy_hbm, bathy_in), (rhs_hbm, rhs_in), (pressure_hbm, pressure_in))
        )
    ]
    for load in loads:
        load.start()

    def clear(ref, level):
        for k in range(level.k):
            ref[k, 0:BASE, :] = jnp.zeros((BASE, LANES), jnp.float32)
            tail = level.alloc - BASE - level.n
            ref[k, BASE + level.n : level.alloc, :] = jnp.zeros((tail, LANES), jnp.float32)

    clear(g_ref, fine)
    for i, level in enumerate(levels):
        for refs in (w_refs, s_refs, v_refs, south_refs, u_refs):
            clear(refs[i], level)

    top = slice(BASE, BASE + HALO)
    middle = slice(BASE + HALO, BASE + HALO + rows)
    bottom = slice(BASE + HALO + rows, BASE + 2 * HALO + rows)
    half = rows // 2 ** (LEVELS + 1)

    def blank(ref, *index):
        ref[index] = jnp.zeros(ref.at[index].shape, jnp.float32)

    @pl.when(at_west)
    def _():
        blank(got_west, slice(None), slice(None))
        blank(wide, slice(None), 0)

    @pl.when(at_east)
    def _():
        blank(got_east, slice(None), slice(None))
        blank(wide, slice(None), 2)

    for edge, strip, wide_strip in ((at_north, top, slice(0, half)), (at_south, bottom, slice(3 * half, 4 * half))):

        @pl.when(edge)
        def _():
            blank(got_west, strip, slice(None))
            blank(got_east, strip, slice(None))
            blank(fields, slice(None), slice(0, 2), strip)
            blank(wide, slice(None), slice(None), wide_strip)

    for load in loads:
        load.wait()

    first = BASE + HALO

    prep = rows
    lane = lane_of((prep, LANES))

    def prepare(i, carry):
        at = i * prep
        to = first + i * prep
        made = []
        for k in range(2):
            part = slice(k * LANES, (k + 1) * LANES)
            wet = wet_in[pl.ds(at, prep), part].astype(jnp.float32)
            bathy = bathy_in[pl.ds(at, prep), part].astype(jnp.float32)
            w = wet * (1.0 + 0.5 * bathy)
            s = wet * rhs_in[pl.ds(at, prep), part]
            g = wet * pressure_in[pl.ds(at, prep), part]
            fields[0, k, pl.ds(to, prep), :] = w
            fields[1, k, pl.ds(to, prep), :] = s
            fields[2, k, pl.ds(to, prep), :] = g
            made.append((w, s, g))
        w, s, g = made[1]
        packed = jnp.where(lane >= LANES - HALO, w, pltpu.roll(s, LANES - HALO, 1))
        pack_east[pl.ds(at, prep), :] = jnp.where(
            lane >= LANES - 2 * HALO, packed, pltpu.roll(g, LANES - 2 * HALO, 1)
        )
        w, s, g = made[0]
        packed = jnp.where(lane < HALO, w, pltpu.roll(s, HALO, 1))
        pack_west[pl.ds(at, prep), :] = jnp.where(lane < 2 * HALO, packed, pltpu.roll(g, 2 * HALO, 1))
        return carry

    prepare(0, 0)

    count = lambda low, high: 3 - low.astype(jnp.int32) - high.astype(jnp.int32)
    pl.semaphore_wait(barrier, count(at_north, at_south) * count(at_west, at_east) - 1)

    head, tail = slice(0, HALO), slice(rows - HALO, rows)
    mine_head = slice(first, first + HALO)
    mine_tail = slice(first + rows - HALO, first + rows)
    strips = [
        (pack_east, got_west.at[middle]),
        (pack_west, got_east.at[middle]),
        (fields.at[:, 0:2, mine_tail], fields.at[:, 0:2, top]),
        (fields.at[:, 0:2, mine_head], fields.at[:, 0:2, bottom]),
        (pack_east.at[tail], got_west.at[top]),
        (pack_east.at[head], got_west.at[bottom]),
        (pack_west.at[tail], got_east.at[top]),
        (pack_west.at[head], got_east.at[bottom]),
    ]
    copies = [
        pltpu.make_async_remote_copy(
            src_ref=src,
            dst_ref=dst,
            send_sem=send_sem.at[i],
            recv_sem=recv_sem.at[i],
            device_id=around[i],
            device_id_type=MESH,
        )
        for i, (src, dst) in enumerate(strips)
    ]
    start_all(copies)
    wait_all(copies)

    part = fine.n
    lane_part = lane_of((part, LANES))

    def unpack(i, carry):
        at = BASE + i * part
        a = got_west[pl.ds(at, part), :]
        b = got_east[pl.ds(at, part), :]
        left = lane_part >= LANES // 2
        w = jnp.where(lane_part < HALO, b, 0.0)
        fields[0, 2, pl.ds(at, part), :] = jnp.where(lane_part >= LANES - HALO, a, w)
        fields[1, 2, pl.ds(at, part), :] = jnp.where(
            left, pltpu.roll(a, HALO, 1), pltpu.roll(b, LANES - HALO, 1)
        )
        fields[2, 2, pl.ds(at, part), :] = jnp.where(
            left, pltpu.roll(a, 2 * HALO, 1), pltpu.roll(b, LANES - 2 * HALO, 1)
        )
        return carry

    unpack(0, 0)

    def restrict_map(level, coarse_cols, k_in, first_in, scale):
        shape = (k_in * LANES, LANES)
        hit = (level.columns(shape, 0, first_in * LANES) >> 1) == coarse_cols(shape)
        return jnp.where(hit, scale, 0.0).astype(jnp.bfloat16)

    def restrict_plan(l):
        if l == 0:
            return [(0, 2, 0), (2, 1, 1)]
        return [(0, levels[l].k, 0)]

    def restrict(ref, l, start, count, scale, coarse_cols):
        out = []
        for k0, k_in, k_out in restrict_plan(l):
            sums = [
                ref[k, pl.ds(start, count, stride=2), :] + ref[k, pl.ds(start + 1, count, stride=2), :]
                for k in range(k0, k0 + k_in)
            ]
            x = sums[0] if k_in == 1 else jnp.concatenate(sums, axis=1)
            matrix = restrict_map(levels[l], functools.partial(coarse_cols, k_out), k_in, k0, scale)
            out.append(split_dot(x, matrix))
        return out

    def coarse_columns(l):
        if l == LEVELS - 1:
            return lambda k, shape: lax.broadcasted_iota(jnp.int32, shape, 1) & (cols // 2**LEVELS - 1)
        return lambda k, shape: levels[l + 1].columns(shape, 1, k * LANES)

    tile_rows = rows // 2**LEVELS

    def send_tile(f):
        all_rows, up_rows, down_rows = slice(0, tile_rows), slice(0, half), slice(half, tile_rows)
        mid, above, below = slice(half, half + tile_rows), slice(0, half), slice(half + tile_rows, 2 * tile_rows)
        plan = [
            (all_rows, 0, mid),
            (all_rows, 2, mid),
            (down_rows, 1, above),
            (up_rows, 1, below),
            (down_rows, 0, above),
            (up_rows, 0, below),
            (down_rows, 2, above),
            (up_rows, 2, below),
        ]
        out = [
            pltpu.make_async_remote_copy(
                src_ref=own.at[f, src],
                dst_ref=wide.at[f, which, dst],
                send_sem=send2_sem.at[f, i],
                recv_sem=recv2_sem.at[f, i],
                device_id=around[i],
                device_id_type=MESH,
            )
            for i, (src, which, dst) in enumerate(plan)
        ]
        start_all(out)
        return out

    for l in range(LEVELS - 1):
        level = levels[l]
        made = restrict(w_refs[l], l, BASE, level.n // 2, 0.125, coarse_columns(l))
        for k in range(levels[l + 1].k):
            w_refs[l + 1][k, pl.ds(BASE, level.n // 2), :] = made[k]
    last = levels[LEVELS - 1]
    tile = restrict(
        w_refs[LEVELS - 1], LEVELS - 1, BASE + last.ext, tile_rows, 0.125, coarse_columns(LEVELS - 1)
    )[0]
    own[0, :, :] = tile
    wide[0, 1, pl.ds(tile_rows // 2, tile_rows), :] = tile
    weight_copies = send_tile(0)

    def chunk_of(level):
        return level.steps

    for l in range(LEVELS):
        level = levels[l]
        k_count = level.k
        n = chunk_of(level)

        def smooth(at):
            up, down, right, left, diagonal = edges_and_diagonal(w_refs[l], k_count, at, n)
            for k in range(k_count):
                inverse = RELAX / diagonal[k]
                inv_refs[l][k, pl.ds(at, n), :] = inverse
                east_refs[l][k, pl.ds(at, n), :] = right[k]
                south_refs[l][k, pl.ds(at, n), :] = down[k]
                if l > 0:
                    v_refs[l][k, pl.ds(at, n), :] = inverse * s_refs[l][k, pl.ds(at, n), :]
            if l == 0:
                g = [g_ref[k, pl.ds(at, n), :] for k in range(k_count)]
                beside = from_east(g)
                flow = [right[k] * (beside[k] - g[k]) for k in range(k_count)]
                back = from_west(flow)
                for k in range(k_count):
                    below = down[k] * (g_ref[k, pl.ds(at + 1, n), :] - g[k])
                    above = up[k] * (g_ref[k, pl.ds(at - 1, n), :] - g[k])
                    inner = s_refs[0][k, pl.ds(at, n), :] - DAMPING * g[k]
                    total = inner + (flow[k] - back[k]) + (below + above)
                    v_refs[0][k, pl.ds(at, n), :] = g[k] + (RELAX / diagonal[k]) * total

        over_rows(level.steps, n, smooth)

        def to_residual(at):
            out, _ = residual(v_refs[l], s_refs[l], east_refs[l], south_refs[l], k_count, at, n)
            for k in range(k_count):
                u_refs[l][k, pl.ds(at, n), :] = out[k]

        over_rows(level.steps, n, to_residual)
        if l < LEVELS - 1:
            made = restrict(u_refs[l], l, BASE, level.n // 2, 0.25, coarse_columns(l))
            for k in range(levels[l + 1].k):
                s_refs[l + 1][k, pl.ds(BASE, level.n // 2), :] = made[k]
        else:
            tile = restrict(u_refs[l], l, BASE + last.ext, tile_rows, 0.25, coarse_columns(l))[0]
            own[1, :, :] = tile
            wide[1, 1, pl.ds(tile_rows // 2, tile_rows), :] = tile
    source_copies = send_tile(1)

    wait_all(weight_copies)
    tile_cols = cols // 2**LEVELS
    wide_rows = 2 * tile_rows
    lane_wide = lane_of((wide_rows, LANES))

    def merged(f):
        x = jnp.where(lane_wide < 2 * tile_cols, wide[f, 2], 0.0)
        x = jnp.where(lane_wide < tile_cols, wide[f, 1], x)
        return jnp.where(lane_wide >= LANES - tile_cols, wide[f, 0], x)

    w = merged(0)

    def roll_rows(x, shift):
        return pltpu.roll(x, shift % wide_rows, 0)

    c_south = jnp.minimum(w, roll_rows(w, -1))
    c_north = roll_rows(c_south, 1)
    c_east = jnp.minimum(w, pltpu.roll(w, LANES - 1, 1))
    c_west = pltpu.roll(c_east, 1, 1)
    inverse = RELAX / (DAMPING + (c_south + c_north) + (c_east + c_west))
    wait_all(source_copies)
    source = merged(1) * inverse
    a_south, a_north, a_east, a_west = (c * inverse for c in (c_south, c_north, c_east, c_west))

    def sweep(current):
        rows_part = a_south * roll_rows(current, -1) + a_north * roll_rows(current, 1)
        lanes_part = a_east * pltpu.roll(current, LANES - 1, 1) + a_west * pltpu.roll(current, 1, 1)
        return ((1.0 - RELAX) * current + source) + (rows_part + lanes_part)

    current = source
    for _ in range(SWEEPS - 1):
        current = sweep(current)

    for l in range(LEVELS - 1, -1, -1):
        level = levels[l]
        k_count = level.k
        n = chunk_of(level)
        if l == LEVELS - 1:
            lead = (level.ext + 1) // 2
            count = (level.n + 2) // 2
            wide[0, 0, :, :] = current
            coarse = [wide[0, 0, pl.ds(tile_rows // 2 - lead, count), :]]
            start = BASE + level.ext - 2 * lead
            coarse_col = lambda shape: column(shape, 0, 0, LANES // 2, LANES)
            plan = [(0, 1, 0)]
        else:
            count = level.n // 2
            coarse = [v_refs[l + 1][k, pl.ds(BASE, count), :] for k in range(levels[l + 1].k)]
            start = BASE
            plan = [(0, 2, 0), (2, 1, 1)] if l == 0 else [(0, k_count, None)]
        for k0, k_out, k_from in plan:
            if l < LEVELS - 1:
                source_level = levels[l + 1]
                if k_from is None:
                    x = coarse[0] if len(coarse) == 1 else jnp.concatenate(coarse, axis=1)
                    first_lane = 0
                else:
                    x, first_lane = coarse[k_from], k_from * LANES
                coarse_col = lambda shape: source_level.columns(shape, 0, first_lane)
            else:
                x = coarse[0]
            shape = (x.shape[1], k_out * LANES)
            hit = (level.columns(shape, 1, k0 * LANES) >> 1) == coarse_col(shape)
            spread = split_dot(x, jnp.where(hit, 1.0, 0.0).astype(jnp.bfloat16))
            for k in range(k_out):
                add = spread[:, k * LANES : (k + 1) * LANES]
                for side in range(2):
                    at = pl.ds(start + side, count, stride=2)
                    u_refs[l][k0 + k, at, :] = v_refs[l][k0 + k, at, :] + add

        def correct(at):
            out, v = residual(u_refs[l], s_refs[l], east_refs[l], south_refs[l], k_count, at, n)
            for k in range(k_count):
                v_refs[l][k, pl.ds(at, n), :] = v[k] + inv_refs[l][k, pl.ds(at, n), :] * out[k]

        over_rows(level.steps, n, correct)


def finish(field, fields, east_ref, south_ref, out_hbm, res_hbm, res, sem):
    first = BASE + HALO
    rows = out_hbm.shape[0]
    copies = []

    def send(src, hbm, at, n, k):
        copies.append(pltpu.make_async_copy(src, hbm.at[at : at + n, k * LANES : (k + 1) * LANES], sem.at[len(copies)]))
        copies[-1].start()

    for k in range(2):
        send(field.at[k, first : first + rows], out_hbm, 0, rows, k)
    n = rows // PIECES
    for at in range(0, rows, n):
        out, _ = residual(field, fields.at[1], east_ref, south_ref, 3, first + at, n)
        for k in range(2):
            res[k, at : at + n, :] = out[k]
        for k in range(2):
            send(res.at[k, at : at + n], res_hbm, at, n, k)
    for copy in copies:
        copy.wait()


def local(grid_rows, grid_cols, rhs, pressure, wet_mask, bathy_class):
    rows, cols = rhs.shape
    levels = [Level(rows >> l, cols >> l, HALO >> l) for l in range(LEVELS)]
    f32 = jnp.float32
    vmem = lambda *shape: pltpu.VMEM(shape, f32)
    per_level = [vmem(level.k, level.alloc, LANES) for level in levels]
    tile_rows = rows // 2**LEVELS
    scratch = [
        vmem(rows, cols),
        vmem(rows, cols),
        pltpu.VMEM((rows, cols), jnp.int32),
        pltpu.VMEM((rows, cols), jnp.int32),
        vmem(rows, LANES),
        vmem(rows, LANES),
        vmem(levels[0].alloc, LANES),
        vmem(levels[0].alloc, LANES),
        *per_level[1:],
        *per_level[1:],
        *per_level[1:],
        *per_level,
        *per_level[1:],
        *per_level[1:],
        *per_level,
        vmem(2, tile_rows, LANES),
        vmem(2, 3, 2 * tile_rows, LANES),
        pltpu.SemaphoreType.DMA((4,)),
        pltpu.SemaphoreType.DMA((8,)),
        pltpu.SemaphoreType.DMA((8,)),
        pltpu.SemaphoreType.DMA((2, 8)),
        pltpu.SemaphoreType.DMA((2, 8)),
    ]
    block = (levels[0].k, levels[0].alloc, LANES)
    struct = lambda *shape: jax.ShapeDtypeStruct(shape, f32)
    held = pl.pallas_call(
        functools.partial(kernel, grid_rows, grid_cols, levels),
        out_shape=[struct(*block), struct(3, *block), struct(*block), struct(*block)],
        in_specs=[pl.BlockSpec(memory_space=pltpu.HBM)] * 4,
        out_specs=[pl.BlockSpec(memory_space=pltpu.VMEM)] * 4,
        scratch_shapes=scratch,
        compiler_params=pltpu.CompilerParams(
            collective_id=0, has_side_effects=True, vmem_limit_bytes=40 * 1024 * 1024
        ),
    )(*[pltpu.with_memory_space_constraint(x, pltpu.HBM) for x in (rhs, pressure, wet_mask, bathy_class)])
    return pl.pallas_call(
        finish,
        out_shape=[struct(rows, cols)] * 2,
        in_specs=[pl.BlockSpec(memory_space=pltpu.VMEM)] * 4,
        out_specs=[pl.BlockSpec(memory_space=pltpu.HBM)] * 2,
        scratch_shapes=[vmem(2, rows, LANES), pltpu.SemaphoreType.DMA((2 + 2 * PIECES,))],
        compiler_params=pltpu.CompilerParams(vmem_limit_bytes=48 * 1024 * 1024),
    )(*held)


def solution(mesh):
    placed = P("gx", "gy")
    body = functools.partial(local, mesh.shape["gx"], mesh.shape["gy"])
    return jax.shard_map(
        lambda *args: tuple(body(*args)),
        mesh=mesh,
        in_specs=(placed,) * 4,
        out_specs=(placed,) * 2,
        check_vma=False,
    )
```
